512 devices in a mesh: img: 8 (over z), neu: 64 (over x, y, core).
Axes of the slice: x: 4, y: 8, z: 8, core: 2. Of those that a mesh axis runs over, the one named last changes fastest.
Arguments:
- image_values: bfloat16 [4096, 4096], P('neu', 'img'), may hold values from 0.25 to 16
- image_mask: int32 [4096, 4096], P('neu', 'img'), may hold values 0 or 1
- weights: bfloat16 [3, 4096, 4, 8], P(None, 'neu'), may hold values from -0.25 to 0.34960938
- block_index: int32 [3, 128, 4], P(None, 'neu'), may hold values from 0 to 511, as said below
Outputs:
- activations: bfloat16 [4096, 4096], P('neu', 'img')
- row_sums: float32 [4096], P(('img', 'neu'))
The draws below stay inside these ranges and needn't reach their ends.
Inputs may be any that keep to these rules, and one draw needn't show every extreme that they name: Split the 512 input blocks into 64 runs of consecutive blocks, and the 128 output blocks likewise; if output block b lies in run s, block_index[l, b, k] lies in run (s + k * 16 + l) mod 64.
All inputs are finite; a program needn't handle non-finite values. No bound on the sum of `image_mask` on one device may be relied on, other than what follows from the above.
Results may differ from the reference program's by a relative error of at most 0.0035.
Values may be sent and summed in bfloat16 or wider, within the bound.
No kernel may reach another device: no remote copies, remote signals or barrier semaphores. Data moves between devices by JAX's collectives and lax.ppermute only.
A program may use at most 64 MiB of HBM per device.

```python
import math
import jax
import jax.numpy as jnp

NEU = 4096
LAYERS = 3
KB = 4
IB = 8
OB = 32
IMAGES = 4096
NOB = 128
N_NEU = 64


def draw_block_index(key, part):
    per_run = NEU // IB // N_NEU
    outs_per_run = NOB // N_NEU
    owner = jnp.arange(NOB, dtype=jnp.int32) // outs_per_run
    layer_ids = jnp.arange(LAYERS, dtype=jnp.int32)
    slot_ids = jnp.arange(KB, dtype=jnp.int32)
    source = (owner[None, :, None] + slot_ids[None, None, :] * (N_NEU // KB) + layer_ids[:, None, None]) % N_NEU
    inner = jax.random.randint(jax.random.fold_in(key, 7), (LAYERS, NOB, KB), 0, per_run, dtype=jnp.int32)
    return (source * per_run + inner).astype(jnp.int32)


def place_ends(values, stream_key, low, high):
    extent = values.shape
    index_at = [jax.random.randint(jax.random.fold_in(stream_key, axis), (), 0, extent[axis]) for axis in range(len(extent))]
    values = values.at[tuple(index_at)].set(low)
    longest = extent.index(max(extent))
    index_at[longest] = (index_at[longest] + 1) % extent[longest]
    return values.at[tuple(index_at)].set(high)


def block_scale(stream_key, extent, pieces, least, high):
    factor_of, own = 1.0, jax.random.fold_in(stream_key, 6)
    for dim, blocks in pieces:
        draws = jnp.exp(jax.random.uniform(jax.random.fold_in(own, dim), (blocks,), jnp.float32, least / len(pieces), high / len(pieces)))
        factor_of = factor_of * jnp.repeat(draws, extent[dim] // blocks).reshape([-1 if axis == dim else 1 for axis in range(len(extent))])
    return factor_of


def setup_inputs(seed: int = 0) -> dict:
    splits = jax.random.split(jax.random.key(seed), 5)
    return {
        "image_values": jnp.clip(jnp.exp(math.log(16.0) - 4.158883 * jax.random.uniform(splits[0], (NEU, IMAGES), jnp.float32) ** block_scale(splits[0], (NEU, IMAGES), ((0, 64), (1, 8)), -0.2, 0.2)), 0.25, 16.0).astype(jnp.bfloat16),
        "image_mask": place_ends((jax.random.randint(splits[1], (NEU, IMAGES), 0, 2) < 1).astype(jnp.int32), jax.random.fold_in(splits[1], 1), 0, 1),
        "weights": jnp.clip(-0.25 + 0.5996094 * jax.random.uniform(splits[2], (LAYERS, NEU, KB, IB), jnp.float32) ** block_scale(splits[2], (LAYERS, NEU, KB, IB), ((1, 64),), -0.2, 0.2), -0.25, 0.34960938).astype(jnp.bfloat16),
        "block_index": draw_block_index(jax.random.fold_in(splits[4], 71), 0),
    }


bias_value = 0.35
ceiling = 32.0


def advance(activity, layer_weights, layer_blocks):
    offsets = jnp.arange(IB, dtype=jnp.int32)
    rows_wanted = (layer_blocks.astype(jnp.int32)[:, :, None] * IB + offsets[None, None, :]).reshape(-1)
    picked = jnp.take(activity, rows_wanted, axis=0).reshape(layer_blocks.shape[0], KB * IB, -1).astype(jnp.float32)
    weights_full = layer_weights.reshape(layer_blocks.shape[0], OB, KB * IB).astype(jnp.float32)
    summed = jnp.einsum("dom,dmr->dor", weights_full, picked)
    clamped = jnp.minimum(jnp.maximum(summed - bias_value, 0.0), ceiling)
    return clamped.astype(jnp.bfloat16).reshape(NEU, -1)


def reference(image_values, image_mask, weights, block_index):
    activity = image_values * image_mask.astype(jnp.bfloat16)
    for layer_number in range(LAYERS):
        activity = advance(activity, weights[layer_number], block_index[layer_number])
    totals = jnp.sum(activity.astype(jnp.float32), axis=0)
    return activity, totals
```

```python
import jax
import jax.numpy as jnp
from jax import lax
from jax.experimental import pallas as pl
from jax.experimental.pallas import tpu as pltpu
from jax.sharding import PartitionSpec as P

KB = 4
IB = 8
OB = 32
LANES = 128

bias_value = 0.35
ceiling = 32.0


def from_ahead(block, axis, distance):
    devices = lax.axis_size(axis)
    route = [((i + distance) % devices, i) for i in range(devices)]
    return lax.ppermute(block, axis, route)


def pack_kernel(values_ref, mask_ref, weights_ref, index_ref, first_ref, second_ref, third_ref):
    rows, columns = values_ref.shape
    outs = weights_ref.shape[-1]
    half = KB * outs
    run_blocks = rows // IB
    first_ref[0:rows, :] = values_ref[...] * mask_ref[...].astype(jnp.float32).astype(jnp.bfloat16)
    block_of_lane = lax.broadcasted_iota(jnp.int32, (IB, half), 1) // OB
    for layer in range(3):
        table = jnp.concatenate([weights_ref[layer, k].astype(jnp.float32) for k in range(KB)], axis=1)
        inner = jnp.zeros((IB, half), jnp.int32)
        for k in range(KB):
            for d in range(outs // OB):
                lane_block = k * (outs // OB) + d
                inner = jnp.where(block_of_lane == lane_block, index_ref[layer, d, k] % run_blocks, inner)
        packed = jnp.concatenate([table, inner.astype(jnp.float32)], axis=1).astype(jnp.bfloat16)
        if layer == 0:
            first_ref[rows : rows + IB, :] = packed
        elif layer == 1:
            second_ref[...] = packed
        else:
            third_ref[...] = packed


def dense_transposed(gathered_ref, table_row, outs, positions, run_blocks):
    half = KB * outs
    tables = [gathered_ref[p, table_row : table_row + IB, :].astype(jnp.float32) for p in range(positions)]
    rows = []
    for source in range(positions):
        w_parts, i_parts = [], []
        for target in range(positions):
            k = (source - target) % positions
            w_parts.append(tables[target][:, k * outs : (k + 1) * outs])
            i_parts.append(tables[target][:, half + k * outs : half + (k + 1) * outs])
        w_row = jnp.concatenate(w_parts, axis=1)
        i_row = jnp.concatenate(i_parts, axis=1)
        for b in range(run_blocks):
            rows.append(jnp.where(i_row == float(b), w_row, 0.0))
    return jnp.concatenate(rows, axis=0).astype(jnp.bfloat16)


def advance(dense_t, activity):
    summed = lax.dot_general(
        dense_t, activity, (((0,), (0,)), ((), ())), preferred_element_type=jnp.float32
    )
    return jnp.minimum(jnp.maximum(summed - bias_value, 0.0), ceiling).astype(jnp.bfloat16)


def layers_kernel(place_ref, gathered_ref, activations_ref, sums_ref, last_ref, totals_ref):
    positions, _, columns = gathered_ref.shape
    rows = activations_ref.shape[0]
    run_blocks = rows // IB
    activity = jnp.concatenate([gathered_ref[p, 0:rows, :] for p in range(positions)], axis=0)
    for layer in range(3):
        dense_t = dense_transposed(gathered_ref, rows + layer * IB, rows, positions, run_blocks)
        activity = advance(dense_t, activity)
    last_ref[...] = activity.reshape(positions, rows, columns)
    activations_ref[...] = last_ref[place_ref[0]]
    totals = jnp.sum(activity.astype(jnp.float32), axis=0, keepdims=True)
    share = columns // positions
    for p in range(positions):
        totals_ref[p] = totals[:, p * share : (p + 1) * share]
    sums_ref[...] = jnp.broadcast_to(totals_ref[place_ref[0]][None], sums_ref.shape)


def on_device(image_values, image_mask, weights, block_index):
    rows, columns = image_values.shape
    devices = lax.axis_size("neu")
    stride = devices // KB
    layer_count = weights.shape[0]
    vmem = pl.BlockSpec(memory_space=pltpu.VMEM)
    smem = pl.BlockSpec(memory_space=pltpu.SMEM)
    first, second, third = pl.pallas_call(
        pack_kernel,
        in_specs=[vmem, vmem, vmem, smem],
        out_specs=[vmem, vmem, vmem],
        out_shape=[
            jax.ShapeDtypeStruct((rows + IB, columns), jnp.bfloat16),
            jax.ShapeDtypeStruct((IB, columns), jnp.bfloat16),
            jax.ShapeDtypeStruct((IB, columns), jnp.bfloat16),
        ],
        name="pack",
    )(image_values, image_mask, weights.transpose(0, 2, 3, 1), block_index)
    first = from_ahead(first, "neu", 3)
    second = from_ahead(second, "neu", 2)
    message = jnp.concatenate([first, second, third], axis=0)
    along_x = [[p * stride + g for p in range(KB)] for g in range(stride)]
    gathered = lax.all_to_all(
        jnp.broadcast_to(message[None], (KB, *message.shape)), "neu", 0, 0, axis_index_groups=along_x, tiled=True
    )
    me = lax.axis_index("neu")
    share = columns // KB
    activations, sums = pl.pallas_call(
        layers_kernel,
        in_specs=[smem, vmem],
        out_specs=[vmem, vmem],
        out_shape=[
            jax.ShapeDtypeStruct((rows, columns), jnp.bfloat16),
            jax.ShapeDtypeStruct((stride, 1, share), jnp.float32),
        ],
        scratch_shapes=[
            pltpu.VMEM((KB, rows, columns), jnp.bfloat16),
            pltpu.VMEM((KB, 1, share), jnp.float32),
        ],
        name="layers",
    )((me // stride).astype(jnp.int32).reshape(1), gathered)
    across = [[p * stride + g for g in range(stride)] for p in range(KB)]
    parts = lax.all_to_all(sums, "neu", 0, 0, axis_index_groups=across, tiled=True)
    own = columns // devices
    totals = lax.dynamic_slice(jnp.sum(parts, axis=(0, 1)), ((me % stride) * own,), (own,))
    return activations, totals


def solution(mesh):
    in_specs = (P("neu", "img"), P("neu", "img"), P(None, "neu", None, None), P(None, "neu", None))
    out_specs = (P("neu", "img"), P(("img", "neu")))
    return jax.shard_map(
        on_device, mesh=mesh, in_specs=in_specs, out_specs=out_specs, check_vma=False
    )
```

```python
import jax
import jax.numpy as jnp
from jax import lax
from jax.experimental import pallas as pl
from jax.experimental.pallas import tpu as pltpu
from jax.sharding import PartitionSpec as P

KB = 4
IB = 8
OB = 32
LANES = 128

bias_value = 0.35
ceiling = 32.0


def from_ahead(block, axis, distance):
    devices = lax.axis_size(axis)
    route = [((i + distance) % devices, i) for i in range(devices)]
    return lax.ppermute(block, axis, route)


def pack_kernel(values_ref, mask_ref, weights_ref, index_ref, first_ref, second_ref, third_ref):
    rows, columns = values_ref.shape
    outs = weights_ref.shape[-1]
    half = KB * outs
    run_blocks = rows // IB
    first_ref[0:rows, :] = values_ref[...] * mask_ref[...].astype(jnp.float32).astype(jnp.bfloat16)
    block_of_lane = lax.broadcasted_iota(jnp.int32, (IB, half), 1) // OB
    for layer in range(3):
        table = jnp.concatenate([weights_ref[layer, k].astype(jnp.float32) for k in range(KB)], axis=1)
        inner = jnp.zeros((IB, half), jnp.int32)
        for k in range(KB):
            for d in range(outs // OB):
                lane_block = k * (outs // OB) + d
                inner = jnp.where(block_of_lane == lane_block, index_ref[layer, d, k] % run_blocks, inner)
        packed = jnp.concatenate([table, inner.astype(jnp.float32)], axis=1).astype(jnp.bfloat16)
        if layer == 0:
            first_ref[rows : rows + IB, :] = packed
        elif layer == 1:
            second_ref[...] = packed
        else:
            third_ref[...] = packed


def dense_transposed(gathered_ref, table_row, outs, positions, run_blocks):
    half = KB * outs
    tables = [gathered_ref[p, table_row : table_row + IB, :].astype(jnp.float32) for p in range(positions)]
    rows = []
    for source in range(positions):
        w_parts, i_parts = [], []
        for target in range(positions):
            k = (source - target) % positions
            w_parts.append(tables[target][:, k * outs : (k + 1) * outs])
            i_parts.append(tables[target][:, half + k * outs : half + (k + 1) * outs])
        w_row = jnp.concatenate(w_parts, axis=1)
        i_row = jnp.concatenate(i_parts, axis=1)
        for b in range(run_blocks):
            rows.append(jnp.where(i_row == float(b), w_row, 0.0))
    return jnp.concatenate(rows, axis=0).astype(jnp.bfloat16)


def advance(dense_t, activity):
    summed = lax.dot_general(
        dense_t, activity, (((0,), (0,)), ((), ())), preferred_element_type=jnp.float32
    )
    return jnp.minimum(jnp.maximum(summed - bias_value, 0.0), ceiling).astype(jnp.bfloat16)


def layers_kernel(place_ref, gathered_ref, activations_ref, sums_ref, last_ref, totals_ref):
    positions, _, columns = gathered_ref.shape
    rows = activations_ref.shape[0]
    run_blocks = rows // IB
    activity = jnp.concatenate([gathered_ref[p, 0:rows, :] for p in range(positions)], axis=0)
    for layer in range(3):
        dense_t = dense_transposed(gathered_ref, rows + layer * IB, rows, positions, run_blocks)
        activity = advance(dense_t, activity)
    last_ref[...] = activity.reshape(positions, rows, columns)
    activations_ref[...] = last_ref[place_ref[0]]
    totals = jnp.sum(activity.astype(jnp.float32), axis=0, keepdims=True)
    share = columns // positions
    for p in range(positions):
        totals_ref[p] = totals[:, p * share : (p + 1) * share]
    sums_ref[...] = jnp.broadcast_to(totals_ref[place_ref[0]][None], sums_ref.shape)


def on_device(image_values, image_mask, weights, block_index):
    rows, columns = image_values.shape
    devices = lax.axis_size("neu")
    stride = devices // KB
    layer_count = weights.shape[0]
    vmem = pl.BlockSpec(memory_space=pltpu.VMEM)
    smem = pl.BlockSpec(memory_space=pltpu.SMEM)
    first, second, third = pl.pallas_call(
        pack_kernel,
        in_specs=[vmem, vmem, vmem, smem],
        out_specs=[vmem, vmem, vmem],
        out_shape=[
            pltpu.VMEM((rows + IB, columns), jnp.bfloat16),
            pltpu.VMEM((IB, columns), jnp.bfloat16),
            pltpu.VMEM((IB, columns), jnp.bfloat16),
        ],
        name="pack",
    )(image_values, image_mask, weights.transpose(0, 2, 3, 1), block_index)
    me = lax.axis_index("neu")
    place, begin = me // stride, (me % stride) * (columns // devices)
    first, place, begin = lax.optimization_barrier((first, place, begin))
    first = from_ahead(first, "neu", 3)
    second = from_ahead(second, "neu", 2)
    message = jnp.concatenate([first, second, third], axis=0)
    along_x = [[p * stride + g for p in range(KB)] for g in range(stride)]
    gathered = lax.all_to_all(
        jnp.broadcast_to(message[None], (KB, *message.shape)), "neu", 0, 0, axis_index_groups=along_x, tiled=True
    )
    share = columns // KB
    activations, sums = pl.pallas_call(
        layers_kernel,
        in_specs=[smem, vmem],
        out_specs=[vmem, vmem],
        out_shape=[
            jax.ShapeDtypeStruct((rows, columns), jnp.bfloat16),
            pltpu.VMEM((stride, 1, share), jnp.float32),
        ],
        scratch_shapes=[
            pltpu.VMEM((KB, rows, columns), jnp.bfloat16),
            pltpu.VMEM((KB, 1, share), jnp.float32),
        ],
        name="layers",
    )(place.reshape(1), pltpu.with_memory_space_constraint(gathered, pltpu.VMEM))
    across = [[p * stride + g for g in range(stride)] for p in range(KB)]
    parts = lax.all_to_all(sums, "neu", 0, 0, axis_index_groups=across, tiled=True)
    own = columns // devices
    totals = lax.dynamic_slice(jnp.sum(parts, axis=(0, 1)), (begin,), (own,))
    return activations, totals


def solution(mesh):
    in_specs = (P("neu", "img"), P("neu", "img"), P(None, "neu", None, None), P(None, "neu", None))
    out_specs = (P("neu", "img"), P(("img", "neu")))
    return jax.shard_map(
        on_device, mesh=mesh, in_specs=in_specs, out_specs=out_specs, check_vma=False
    )
```

```python
import jax
import jax.numpy as jnp
from jax import lax
from jax.experimental import pallas as pl
from jax.experimental.pallas import tpu as pltpu
from jax.sharding import PartitionSpec as P

KB = 4
IB = 8
OB = 32
LANES = 128

bias_value = 0.35
ceiling = 32.0


def from_ahead(block, axis, distance):
    devices = lax.axis_size(axis)
    route = [((i + distance) % devices, i) for i in range(devices)]
    return lax.ppermute(block, axis, route)


def pack_kernel(values_ref, mask_ref, weights_ref, index_ref, first_ref, second_ref, third_ref):
    rows, columns = values_ref.shape
    outs = weights_ref.shape[-1]
    half = KB * outs
    run_blocks = rows // IB
    first_ref[0:rows, :] = values_ref[...] * mask_ref[...].astype(jnp.float32).astype(jnp.bfloat16)
    block_of_lane = lax.broadcasted_iota(jnp.int32, (IB, half), 1) // OB
    for layer in range(3):
        table = jnp.concatenate([weights_ref[layer, k].astype(jnp.float32) for k in range(KB)], axis=1)
        inner = jnp.zeros((IB, half), jnp.int32)
        for k in range(KB):
            for d in range(outs // OB):
                lane_block = k * (outs // OB) + d
                inner = jnp.where(block_of_lane == lane_block, index_ref[layer, d, k] % run_blocks, inner)
        packed = jnp.concatenate([table, inner.astype(jnp.float32)], axis=1).astype(jnp.bfloat16)
        if layer == 0:
            first_ref[rows : rows + IB, :] = packed
        elif layer == 1:
            second_ref[...] = packed
        else:
            third_ref[...] = packed


def dense_transposed(gathered_ref, table_row, outs, positions, run_blocks):
    half = KB * outs
    tables = [gathered_ref[p, table_row : table_row + IB, :].astype(jnp.float32) for p in range(positions)]
    rows = []
    for source in range(positions):
        w_parts, i_parts = [], []
        for target in range(positions):
            k = (source - target) % positions
            w_parts.append(tables[target][:, k * outs : (k + 1) * outs])
            i_parts.append(tables[target][:, half + k * outs : half + (k + 1) * outs])
        w_row = jnp.concatenate(w_parts, axis=1)
        i_row = jnp.concatenate(i_parts, axis=1)
        for b in range(run_blocks):
            rows.append(jnp.where(i_row == float(b), w_row, 0.0))
    return jnp.concatenate(rows, axis=0).astype(jnp.bfloat16)


def advance(dense_t, activity):
    summed = lax.dot_general(
        dense_t, activity, (((0,), (0,)), ((), ())), preferred_element_type=jnp.float32
    )
    return jnp.minimum(jnp.maximum(summed - bias_value, 0.0), ceiling).astype(jnp.bfloat16)


def layers_kernel(gathered_ref, activations_ref, sums_ref, last_ref, totals_ref):
    positions, _, columns = gathered_ref.shape
    rows = activations_ref.shape[0]
    run_blocks = rows // IB
    place = lax.axis_index("neu") // (lax.axis_size("neu") // KB)
    activity = jnp.concatenate([gathered_ref[p, 0:rows, :] for p in range(positions)], axis=0)
    for layer in range(3):
        dense_t = dense_transposed(gathered_ref, rows + layer * IB, rows, positions, run_blocks)
        activity = advance(dense_t, activity)
    last_ref[...] = activity.reshape(positions, rows, columns)
    activations_ref[...] = last_ref[place]
    totals = jnp.sum(activity.astype(jnp.float32), axis=0, keepdims=True)
    share = columns // positions
    for p in range(positions):
        totals_ref[p] = totals[:, p * share : (p + 1) * share]
    sums_ref[...] = jnp.broadcast_to(totals_ref[place][None], sums_ref.shape)


def finish_kernel(parts_ref, run_ref, activations_ref, totals_ref, own_ref, copied, summed):
    out = pltpu.make_async_copy(run_ref, activations_ref, copied)
    out.start()
    share = parts_ref.shape[-1]
    own = totals_ref.shape[-1]
    begin = (lax.axis_index("neu") % parts_ref.shape[0]) * own
    totals = jnp.broadcast_to(jnp.sum(parts_ref[...], axis=0), (8, share))
    own_ref[...] = pltpu.roll(totals, share - begin, 1)[0:1, 0:own]
    own_out = pltpu.make_async_copy(own_ref, totals_ref, summed)
    own_out.start()
    out.wait()
    own_out.wait()


def on_device(image_values, image_mask, weights, block_index):
    rows, columns = image_values.shape
    devices = lax.axis_size("neu")
    stride = devices // KB
    layer_count = weights.shape[0]
    vmem = pl.BlockSpec(memory_space=pltpu.VMEM)
    smem = pl.BlockSpec(memory_space=pltpu.SMEM)
    first, second, third = pl.pallas_call(
        pack_kernel,
        in_specs=[vmem, vmem, vmem, smem],
        out_specs=[vmem, vmem, vmem],
        out_shape=[
            pltpu.VMEM((rows + IB, columns), jnp.bfloat16),
            pltpu.VMEM((IB, columns), jnp.bfloat16),
            pltpu.VMEM((IB, columns), jnp.bfloat16),
        ],
        name="pack",
    )(image_values, image_mask, weights.transpose(0, 2, 3, 1), block_index)
    first = from_ahead(first, "neu", 3)
    second = from_ahead(second, "neu", 2)
    message = jnp.concatenate([first, second, third], axis=0)
    along_x = [[p * stride + g for p in range(KB)] for g in range(stride)]
    gathered = lax.all_to_all(
        jnp.broadcast_to(message[None], (KB, *message.shape)), "neu", 0, 0, axis_index_groups=along_x, tiled=True
    )
    share = columns // KB
    activations, sums = pl.pallas_call(
        layers_kernel,
        in_specs=[vmem],
        out_specs=[vmem, vmem],
        out_shape=[
            pltpu.VMEM((rows, columns), jnp.bfloat16),
            pltpu.VMEM((stride, 1, share), jnp.float32),
        ],
        scratch_shapes=[
            pltpu.VMEM((KB, rows, columns), jnp.bfloat16),
            pltpu.VMEM((KB, 1, share), jnp.float32),
        ],
        name="layers",
    )(pltpu.with_memory_space_constraint(gathered, pltpu.VMEM))
    across = [[p * stride + g for g in range(stride)] for p in range(KB)]
    parts = lax.all_to_all(sums, "neu", 0, 0, axis_index_groups=across, tiled=True)
    activations, totals = pl.pallas_call(
        finish_kernel,
        in_specs=[vmem, vmem],
        out_specs=[pl.BlockSpec(memory_space=pl.ANY)] * 2,
        out_shape=[
            jax.ShapeDtypeStruct((rows, columns), jnp.bfloat16),
            jax.ShapeDtypeStruct((1, columns // devices), jnp.float32),
        ],
        scratch_shapes=[
            pltpu.VMEM((1, columns // devices), jnp.float32),
            pltpu.SemaphoreType.DMA(()),
            pltpu.SemaphoreType.DMA(()),
        ],
        name="finish",
    )(
        pltpu.with_memory_space_constraint(parts, pltpu.VMEM),
        pltpu.with_memory_space_constraint(activations, pltpu.VMEM),
    )
    return activations, totals.reshape(-1)


def solution(mesh):
    in_specs = (P("neu", "img"), P("neu", "img"), P(None, "neu", None, None), P(None, "neu", None))
    out_specs = (P("neu", "img"), P(("img", "neu")))
    return jax.shard_map(
        on_device, mesh=mesh, in_specs=in_specs, out_specs=out_specs, check_vma=False
    )
```

```python
import jax
import jax.numpy as jnp
from jax import lax
from jax.experimental import pallas as pl
from jax.experimental.pallas import tpu as pltpu
from jax.sharding import PartitionSpec as P

KB = 4
IB = 8
OB = 32
LANES = 128

bias_value = 0.35
ceiling = 32.0


def from_ahead(block, axis, distance):
    devices = lax.axis_size(axis)
    route = [((i + distance) % devices, i) for i in range(devices)]
    return lax.ppermute(block, axis, route)


def pack_kernel(values_ref, mask_ref, weights_ref, index_ref, first_ref, second_ref, third_ref):
    rows, columns = values_ref.shape
    outs = weights_ref.shape[-1]
    half = KB * outs
    run_blocks = rows // IB
    first_ref[0:rows, :] = values_ref[...] * mask_ref[...].astype(jnp.float32).astype(jnp.bfloat16)
    slot = lax.broadcasted_iota(jnp.int32, (IB, LANES), 0)
    out_block = lax.broadcasted_iota(jnp.int32, (IB, LANES), 1) // OB
    nothing = jnp.zeros((IB, LANES), jnp.float32)
    for layer in range(3):
        table = jnp.concatenate([weights_ref[layer, k].astype(jnp.float32) for k in range(KB)], axis=1)
        inner = jnp.zeros((IB, LANES), jnp.int32)
        for k in range(KB):
            for d in range(outs // OB):
                here = (slot == k + (KB if layer == 1 else 0)) & (out_block == d)
                inner = jnp.where(here, index_ref[layer, d, k] % run_blocks, inner)
        inner = inner.astype(jnp.float32)
        parts = [table, nothing, inner] if layer == 2 else [table, inner, nothing]
        packed = jnp.concatenate(parts, axis=1).astype(jnp.bfloat16)
        if layer == 0:
            first_ref[rows : rows + IB, :] = packed
        elif layer == 1:
            second_ref[...] = packed
        else:
            third_ref[...] = packed


def join_kernel(first_ref, second_ref, third_ref, message_ref):
    rows = first_ref.shape[0] - IB
    half = rows * KB
    for p in range(message_ref.shape[0]):
        message_ref[p, 0:rows, :] = first_ref[0:rows, :]
        message_ref[p, rows : rows + IB, 0:half] = first_ref[rows : rows + IB, 0:half]
        message_ref[p, rows : rows + IB, half:] = second_ref[:, 0:half]
        message_ref[p, rows + IB :, 0:half] = third_ref[:, 0:half]
        message_ref[p, rows + IB :, half : half + LANES] = (
            first_ref[rows : rows + IB, half : half + LANES] + second_ref[:, half : half + LANES]
        )
        message_ref[p, rows + IB :, half + LANES :] = third_ref[:, half + LANES :]


def dense_transposed(gathered_ref, layer, outs, positions, run_blocks):
    half = KB * outs
    table_row, table_lane, index_lane, index_row = (
        (outs, 0, half, 0),
        (outs, half, half, KB),
        (outs + IB, 0, half + LANES, 0),
    )[layer]
    tables = [
        gathered_ref[p, table_row : table_row + IB, table_lane : table_lane + half].astype(jnp.float32)
        for p in range(positions)
    ]
    inner = [
        gathered_ref[p, outs + IB : outs + 2 * IB, index_lane : index_lane + LANES].astype(jnp.float32)
        for p in range(positions)
    ]
    rows = []
    for source in range(positions):
        w_parts, i_parts = [], []
        for target in range(positions):
            k = (source - target) % positions
            w_parts.append(tables[target][:, k * outs : (k + 1) * outs])
            i_parts.append(inner[target][index_row + k : index_row + k + 1, 0:outs])
        w_row = jnp.concatenate(w_parts, axis=1)
        i_row = jnp.broadcast_to(jnp.concatenate(i_parts, axis=1), w_row.shape)
        for b in range(run_blocks):
            rows.append(jnp.where(i_row == float(b), w_row, 0.0))
    return jnp.concatenate(rows, axis=0).astype(jnp.bfloat16)


def advance(dense_t, activity):
    summed = lax.dot_general(
        dense_t, activity, (((0,), (0,)), ((), ())), preferred_element_type=jnp.float32
    )
    return jnp.minimum(jnp.maximum(summed - bias_value, 0.0), ceiling).astype(jnp.bfloat16)


def layers_kernel(gathered_ref, activations_ref, sums_ref, last_ref, totals_ref):
    positions, _, columns = gathered_ref.shape
    rows = activations_ref.shape[0]
    run_blocks = rows // IB
    place = lax.axis_index("neu") // (lax.axis_size("neu") // KB)
    activity = jnp.concatenate([gathered_ref[p, 0:rows, :] for p in range(positions)], axis=0)
    for layer in range(3):
        dense_t = dense_transposed(gathered_ref, layer, rows, positions, run_blocks)
        activity = advance(dense_t, activity)
    last_ref[...] = activity.reshape(positions, rows, columns)
    activations_ref[...] = last_ref[place]
    totals = jnp.sum(activity.astype(jnp.float32), axis=0, keepdims=True)
    share = columns // positions
    for p in range(positions):
        totals_ref[p] = totals[:, p * share : (p + 1) * share]
    sums_ref[...] = jnp.broadcast_to(totals_ref[place][None], sums_ref.shape)


def finish_kernel(parts_ref, run_ref, activations_ref, totals_ref, own_ref, copied, summed):
    out = pltpu.make_async_copy(run_ref, activations_ref, copied)
    out.start()
    share = parts_ref.shape[-1]
    own = totals_ref.shape[-1]
    begin = (lax.axis_index("neu") % parts_ref.shape[0]) * own
    totals = jnp.broadcast_to(jnp.sum(parts_ref[...], axis=0), (8, share))
    own_ref[...] = pltpu.roll(totals, share - begin, 1)[0:1, 0:own]
    own_out = pltpu.make_async_copy(own_ref, totals_ref, summed)
    own_out.start()
    out.wait()
    own_out.wait()


def on_device(image_values, image_mask, weights, block_index):
    rows, columns = image_values.shape
    devices = lax.axis_size("neu")
    stride = devices // KB
    layer_count = weights.shape[0]
    vmem = pl.BlockSpec(memory_space=pltpu.VMEM)
    smem = pl.BlockSpec(memory_space=pltpu.SMEM)
    first, second, third = pl.pallas_call(
        pack_kernel,
        in_specs=[vmem, vmem, vmem, smem],
        out_specs=[vmem, vmem, vmem],
        out_shape=[
            pltpu.VMEM((rows + IB, columns), jnp.bfloat16),
            pltpu.VMEM((IB, columns), jnp.bfloat16),
            pltpu.VMEM((IB, columns), jnp.bfloat16),
        ],
        name="pack",
    )(image_values, image_mask, weights.transpose(0, 2, 3, 1), block_index)
    first = from_ahead(first, "neu", 3)
    second = from_ahead(second, "neu", 2)
    message = pl.pallas_call(
        join_kernel,
        in_specs=[vmem] * 3,
        out_specs=vmem,
        out_shape=pltpu.VMEM((KB, rows + 2 * IB, columns), jnp.bfloat16),
        name="join",
    )(*[pltpu.with_memory_space_constraint(piece, pltpu.VMEM) for piece in (first, second, third)])
    along_x = [[p * stride + g for p in range(KB)] for g in range(stride)]
    gathered = lax.all_to_all(
        message, "neu", 0, 0, axis_index_groups=along_x, tiled=True
    )
    share = columns // KB
    activations, sums = pl.pallas_call(
        layers_kernel,
        in_specs=[vmem],
        out_specs=[vmem, vmem],
        out_shape=[
            pltpu.VMEM((rows, columns), jnp.bfloat16),
            pltpu.VMEM((stride, 1, share), jnp.float32),
        ],
        scratch_shapes=[
            pltpu.VMEM((KB, rows, columns), jnp.bfloat16),
            pltpu.VMEM((KB, 1, share), jnp.float32),
        ],
        name="layers",
    )(pltpu.with_memory_space_constraint(gathered, pltpu.VMEM))
    across = [[p * stride + g for g in range(stride)] for p in range(KB)]
    parts = lax.all_to_all(sums, "neu", 0, 0, axis_index_groups=across, tiled=True)
    activations, totals = pl.pallas_call(
        finish_kernel,
        in_specs=[vmem, vmem],
        out_specs=[pl.BlockSpec(memory_space=pl.ANY)] * 2,
        out_shape=[
            jax.ShapeDtypeStruct((rows, columns), jnp.bfloat16),
            jax.ShapeDtypeStruct((1, columns // devices), jnp.float32),
        ],
        scratch_shapes=[
            pltpu.VMEM((1, columns // devices), jnp.float32),
            pltpu.SemaphoreType.DMA(()),
            pltpu.SemaphoreType.DMA(()),
        ],
        name="finish",
    )(
        pltpu.with_memory_space_constraint(parts, pltpu.VMEM),
        pltpu.with_memory_space_constraint(activations, pltpu.VMEM),
    )
    return activations, totals.reshape(-1)


def solution(mesh):
    in_specs = (P("neu", "img"), P("neu", "img"), P(None, "neu", None, None), P(None, "neu", None))
    out_specs = (P("neu", "img"), P(("img", "neu")))
    return jax.shard_map(
        on_device, mesh=mesh, in_specs=in_specs, out_specs=out_specs, check_vma=False
    )
```

```python
import jax
import jax.numpy as jnp
from jax import lax
from jax.experimental import pallas as pl
from jax.experimental.pallas import tpu as pltpu
from jax.sharding import PartitionSpec as P

KB = 4
IB = 8
OB = 32
LANES = 128

bias_value = 0.35
ceiling = 32.0


def from_group_ahead(block, axis, distance):
    devices = lax.axis_size(axis)
    groups = devices // KB
    route = [(i - i % groups + (i % groups + distance) % groups, i) for i in range(devices)]
    return lax.ppermute(block, axis, route)


def pack_kernel(values_ref, mask_ref, weights_ref, index_ref, first_ref, second_ref, third_ref):
    rows, columns = values_ref.shape
    outs = weights_ref.shape[-1]
    half = KB * outs
    run_blocks = rows // IB
    first_ref[0:rows, :] = values_ref[...] * mask_ref[...].astype(jnp.float32).astype(jnp.bfloat16)
    slot = lax.broadcasted_iota(jnp.int32, (IB, LANES), 0)
    out_block = lax.broadcasted_iota(jnp.int32, (IB, LANES), 1) // OB
    nothing = jnp.zeros((IB, LANES), jnp.float32)
    for layer in range(3):
        table = jnp.concatenate([weights_ref[layer, k].astype(jnp.float32) for k in range(KB)], axis=1)
        inner = jnp.zeros((IB, LANES), jnp.int32)
        for k in range(KB):
            for d in range(outs // OB):
                here = (slot == k + (KB if layer == 1 else 0)) & (out_block == d)
                inner = jnp.where(here, index_ref[layer, d, k] % run_blocks, inner)
        inner = inner.astype(jnp.float32)
        parts = [table, nothing, inner] if layer == 2 else [table, inner, nothing]
        packed = jnp.concatenate(parts, axis=1).astype(jnp.bfloat16)
        if layer == 0:
            first_ref[rows : rows + IB, :] = packed
        elif layer == 1:
            second_ref[...] = packed
        else:
            third_ref[...] = packed


def join_kernel(first_ref, second_ref, third_ref, message_ref):
    rows = first_ref.shape[0] - IB
    half = rows * KB
    for p in range(message_ref.shape[0]):
        message_ref[p, 0:rows, :] = first_ref[0:rows, :]
        message_ref[p, rows : rows + IB, 0:half] = first_ref[rows : rows + IB, 0:half]
        message_ref[p, rows : rows + IB, half:] = second_ref[:, 0:half]
        message_ref[p, rows + IB :, 0:half] = third_ref[:, 0:half]
        message_ref[p, rows + IB :, half : half + LANES] = (
            first_ref[rows : rows + IB, half : half + LANES] + second_ref[:, half : half + LANES]
        )
        message_ref[p, rows + IB :, half + LANES :] = third_ref[:, half + LANES :]


def dense_transposed(gathered_ref, layer, outs, positions, run_blocks):
    half = KB * outs
    table_row, table_lane, index_lane, index_row = (
        (outs, 0, half, 0),
        (outs, half, half, KB),
        (outs + IB, 0, half + LANES, 0),
    )[layer]
    tables = [
        gathered_ref[p, table_row : table_row + IB, table_lane : table_lane + half].astype(jnp.float32)
        for p in range(positions)
    ]
    inner = [
        gathered_ref[p, outs + IB : outs + 2 * IB, index_lane : index_lane + LANES].astype(jnp.float32)
        for p in range(positions)
    ]
    rows = []
    for source in range(positions):
        w_parts, i_parts = [], []
        for target in range(positions):
            k = (source - target) % positions
            w_parts.append(tables[target][:, k * outs : (k + 1) * outs])
            i_parts.append(inner[target][index_row + k : index_row + k + 1, 0:outs])
        w_row = jnp.concatenate(w_parts, axis=1)
        i_row = jnp.broadcast_to(jnp.concatenate(i_parts, axis=1), w_row.shape)
        for b in range(run_blocks):
            rows.append(jnp.where(i_row == float(b), w_row, 0.0))
    return jnp.concatenate(rows, axis=0).astype(jnp.bfloat16)


def advance(dense_t, activity):
    summed = lax.dot_general(
        dense_t, activity, (((0,), (0,)), ((), ())), preferred_element_type=jnp.float32
    )
    return jnp.minimum(jnp.maximum(summed - bias_value, 0.0), ceiling).astype(jnp.bfloat16)


def layers_kernel(gathered_ref, activations_ref, sums_ref, last_ref, totals_ref):
    positions, _, columns = gathered_ref.shape
    rows = activations_ref.shape[0]
    run_blocks = rows // IB
    groups = lax.axis_size("neu") // KB
    place = lax.axis_index("neu") // groups
    group = lax.axis_index("neu") % groups
    wraps = (None, group == groups - 3, group >= groups - 2)
    activity = jnp.concatenate([gathered_ref[p, 0:rows, :] for p in range(positions)], axis=0)
    for layer in range(3):
        dense_t = dense_transposed(gathered_ref, layer, rows, positions, run_blocks)
        if layer > 0:
            further = jnp.concatenate([activity[rows:], activity[:rows]], axis=0)
            activity = jnp.where(wraps[layer], further, activity)
        activity = advance(dense_t, activity)
    last_ref[...] = activity.reshape(positions, rows, columns)
    activations_ref[...] = last_ref[place]
    totals = jnp.sum(activity.astype(jnp.float32), axis=0, keepdims=True)
    share = columns // positions
    for p in range(positions):
        totals_ref[p] = totals[:, p * share : (p + 1) * share]
    sums_ref[...] = jnp.broadcast_to(totals_ref[place][None], sums_ref.shape)


def finish_kernel(parts_ref, run_ref, activations_ref, totals_ref, own_ref, copied, summed):
    out = pltpu.make_async_copy(run_ref, activations_ref, copied)
    out.start()
    share = parts_ref.shape[-1]
    own = totals_ref.shape[-1]
    begin = (lax.axis_index("neu") % parts_ref.shape[0]) * own
    totals = jnp.broadcast_to(jnp.sum(parts_ref[...], axis=0), (8, share))
    own_ref[...] = pltpu.roll(totals, share - begin, 1)[0:1, 0:own]
    own_out = pltpu.make_async_copy(own_ref, totals_ref, summed)
    own_out.start()
    out.wait()
    own_out.wait()


def on_device(image_values, image_mask, weights, block_index):
    rows, columns = image_values.shape
    devices = lax.axis_size("neu")
    stride = devices // KB
    layer_count = weights.shape[0]
    vmem = pl.BlockSpec(memory_space=pltpu.VMEM)
    smem = pl.BlockSpec(memory_space=pltpu.SMEM)
    first, second, third = pl.pallas_call(
        pack_kernel,
        in_specs=[vmem, vmem, vmem, smem],
        out_specs=[vmem, vmem, vmem],
        out_shape=[
            pltpu.VMEM((rows + IB, columns), jnp.bfloat16),
            pltpu.VMEM((IB, columns), jnp.bfloat16),
            pltpu.VMEM((IB, columns), jnp.bfloat16),
        ],
        name="pack",
    )(image_values, image_mask, weights.transpose(0, 2, 3, 1), block_index)
    first = from_group_ahead(first, "neu", 3)
    second = from_group_ahead(second, "neu", 2)
    message = pl.pallas_call(
        join_kernel,
        in_specs=[vmem] * 3,
        out_specs=vmem,
        out_shape=pltpu.VMEM((KB, rows + 2 * IB, columns), jnp.bfloat16),
        name="join",
    )(*[pltpu.with_memory_space_constraint(piece, pltpu.VMEM) for piece in (first, second, third)])
    along_x = [[p * stride + g for p in range(KB)] for g in range(stride)]
    gathered = lax.all_to_all(
        message, "neu", 0, 0, axis_index_groups=along_x, tiled=True
    )
    share = columns // KB
    activations, sums = pl.pallas_call(
        layers_kernel,
        in_specs=[vmem],
        out_specs=[vmem, vmem],
        out_shape=[
            pltpu.VMEM((rows, columns), jnp.bfloat16),
            pltpu.VMEM((stride, 1, share), jnp.float32),
        ],
        scratch_shapes=[
            pltpu.VMEM((KB, rows, columns), jnp.bfloat16),
            pltpu.VMEM((KB, 1, share), jnp.float32),
        ],
        name="layers",
    )(pltpu.with_memory_space_constraint(gathered, pltpu.VMEM))
    across = [[p * stride + g for g in range(stride)] for p in range(KB)]
    parts = lax.all_to_all(sums, "neu", 0, 0, axis_index_groups=across, tiled=True)
    activations, totals = pl.pallas_call(
        finish_kernel,
        in_specs=[vmem, vmem],
        out_specs=[pl.BlockSpec(memory_space=pl.ANY)] * 2,
        out_shape=[
            jax.ShapeDtypeStruct((rows, columns), jnp.bfloat16),
            jax.ShapeDtypeStruct((1, columns // devices), jnp.float32),
        ],
        scratch_shapes=[
            pltpu.VMEM((1, columns // devices), jnp.float32),
            pltpu.SemaphoreType.DMA(()),
            pltpu.SemaphoreType.DMA(()),
        ],
        name="finish",
    )(
        pltpu.with_memory_space_constraint(parts, pltpu.VMEM),
        pltpu.with_memory_space_constraint(activations, pltpu.VMEM),
    )
    return activations, totals.reshape(-1)


def solution(mesh):
    in_specs = (P("neu", "img"), P("neu", "img"), P(None, "neu", None, None), P(None, "neu", None))
    out_specs = (P("neu", "img"), P(("img", "neu")))
    return jax.shard_map(
        on_device, mesh=mesh, in_specs=in_specs, out_specs=out_specs, check_vma=False
    )
```

```python
import jax
import jax.numpy as jnp
from jax import lax
from jax.experimental import pallas as pl
from jax.experimental.pallas import tpu as pltpu
from jax.sharding import PartitionSpec as P

KB = 4
IB = 8
OB = 32
LANES = 128

bias_value = 0.35
ceiling = 32.0


def from_group_ahead(block, axis, distance):
    devices = lax.axis_size(axis)
    groups = devices // KB
    route = [(i - i % groups + (i % groups + distance) % groups, i) for i in range(devices)]
    return lax.ppermute(block, axis, route)


def pack_kernel(values_ref, mask_ref, weights_ref, index_ref, first_ref, second_ref, third_ref):
    rows, columns = values_ref.shape
    outs = weights_ref.shape[-1]
    half = KB * outs
    run_blocks = rows // IB
    first_ref[0:rows, :] = values_ref[...] * mask_ref[...].astype(jnp.float32).astype(jnp.bfloat16)
    slot = lax.broadcasted_iota(jnp.int32, (IB, LANES), 0)
    out_block = lax.broadcasted_iota(jnp.int32, (IB, LANES), 1) // OB
    nothing = jnp.zeros((IB, LANES), jnp.float32)
    for layer in range(3):
        table = jnp.concatenate([weights_ref[layer, k].astype(jnp.float32) for k in range(KB)], axis=1)
        inner = jnp.zeros((IB, LANES), jnp.int32)
        for k in range(KB):
            for d in range(outs // OB):
                here = (slot == k + (KB if layer == 1 else 0)) & (out_block == d)
                inner = jnp.where(here, index_ref[layer, d, k] % run_blocks, inner)
        inner = inner.astype(jnp.float32)
        parts = [table, nothing, inner] if layer == 2 else [table, inner, nothing]
        packed = jnp.concatenate(parts, axis=1).astype(jnp.bfloat16)
        if layer == 0:
            first_ref[rows : rows + IB, :] = packed
        elif layer == 1:
            second_ref[...] = packed
        else:
            third_ref[...] = packed


def join_kernel(first_ref, second_ref, third_ref, message_ref):
    rows = first_ref.shape[0] - IB
    half = rows * KB
    for p in range(message_ref.shape[0]):
        message_ref[p, 0:rows, :] = first_ref[0:rows, :]
        message_ref[p, rows : rows + IB, 0:half] = first_ref[rows : rows + IB, 0:half]
        message_ref[p, rows : rows + IB, half:] = second_ref[:, 0:half]
        message_ref[p, rows + IB :, 0:half] = third_ref[:, 0:half]
        message_ref[p, rows + IB :, half : half + LANES] = (
            first_ref[rows : rows + IB, half : half + LANES] + second_ref[:, half : half + LANES]
        )
        message_ref[p, rows + IB :, half + LANES :] = third_ref[:, half + LANES :]


def dense_transposed(gathered_ref, layer, outs, positions, run_blocks):
    half = KB * outs
    table_row, table_lane, index_lane, index_row = (
        (outs, 0, half, 0),
        (outs, half, half, KB),
        (outs + IB, 0, half + LANES, 0),
    )[layer]
    tables = [
        gathered_ref[p, table_row : table_row + IB, table_lane : table_lane + half].astype(jnp.float32)
        for p in range(positions)
    ]
    inner = [
        gathered_ref[p, outs + IB : outs + 2 * IB, index_lane : index_lane + LANES].astype(jnp.float32)
        for p in range(positions)
    ]
    rows = []
    for source in range(positions):
        w_parts, i_parts = [], []
        for target in range(positions):
            k = (source - target) % positions
            w_parts.append(tables[target][:, k * outs : (k + 1) * outs])
            i_parts.append(inner[target][index_row + k : index_row + k + 1, 0:outs])
        w_row = jnp.concatenate(w_parts, axis=1)
        i_row = jnp.broadcast_to(jnp.concatenate(i_parts, axis=1), w_row.shape)
        for b in range(run_blocks):
            rows.append(jnp.where(i_row == float(b), w_row, 0.0))
    return jnp.concatenate(rows, axis=0).astype(jnp.bfloat16)


def advance(dense_t, activity):
    summed = lax.dot_general(
        dense_t, activity, (((0,), (0,)), ((), ())), preferred_element_type=jnp.float32
    )
    return jnp.minimum(jnp.maximum(summed - bias_value, 0.0), ceiling).astype(jnp.bfloat16)


def layers_kernel(gathered_ref, activations_ref, sums_ref, last_ref, totals_ref):
    positions, _, columns = gathered_ref.shape
    rows = activations_ref.shape[0]
    run_blocks = rows // IB
    groups = lax.axis_size("neu") // KB
    place = lax.axis_index("neu") // groups
    group = lax.axis_index("neu") % groups
    wraps = (None, group == groups - 3, group >= groups - 2)
    activity = jnp.concatenate([gathered_ref[p, 0:rows, :] for p in range(positions)], axis=0)
    for layer in range(3):
        dense_t = dense_transposed(gathered_ref, layer, rows, positions, run_blocks)
        if layer > 0:
            further = jnp.concatenate([activity[rows:], activity[:rows]], axis=0)
            activity = jnp.where(wraps[layer], further, activity)
        activity = advance(dense_t, activity)
    last_ref[...] = activity.reshape(positions, rows, columns)
    activations_ref[...] = last_ref[place]
    totals = jnp.sum(activity.astype(jnp.float32), axis=0, keepdims=True)
    share = columns // positions
    for p in range(positions):
        totals_ref[p] = totals[:, p * share : (p + 1) * share]
    sums_ref[...] = jnp.broadcast_to(totals_ref[place][None], sums_ref.shape)


def finish_kernel(parts_ref, run_ref, activations_ref, totals_ref, own_ref, copied, summed):
    out = pltpu.make_async_copy(run_ref, activations_ref, copied)
    out.start()
    share = parts_ref.shape[-1]
    own = totals_ref.shape[-1]
    begin = (lax.axis_index("neu") % parts_ref.shape[0]) * own
    totals = jnp.broadcast_to(jnp.sum(parts_ref[...], axis=0), (8, share))
    own_ref[...] = pltpu.roll(totals, (share - begin) % share, 1)[0:1, 0:own]
    own_out = pltpu.make_async_copy(own_ref, totals_ref, summed)
    own_out.start()
    out.wait()
    own_out.wait()


def on_device(image_values, image_mask, weights, block_index):
    rows, columns = image_values.shape
    devices = lax.axis_size("neu")
    stride = devices // KB
    layer_count = weights.shape[0]
    vmem = pl.BlockSpec(memory_space=pltpu.VMEM)
    smem = pl.BlockSpec(memory_space=pltpu.SMEM)
    first, second, third = pl.pallas_call(
        pack_kernel,
        in_specs=[vmem, vmem, vmem, smem],
        out_specs=[vmem, vmem, vmem],
        out_shape=[
            pltpu.VMEM((rows + IB, columns), jnp.bfloat16),
            pltpu.VMEM((IB, columns), jnp.bfloat16),
            pltpu.VMEM((IB, columns), jnp.bfloat16),
        ],
        name="pack",
    )(image_values, image_mask, weights.transpose(0, 2, 3, 1), block_index)
    first = from_group_ahead(first, "neu", 3)
    second = from_group_ahead(second, "neu", 2)
    message = pl.pallas_call(
        join_kernel,
        in_specs=[vmem] * 3,
        out_specs=vmem,
        out_shape=pltpu.VMEM((KB, rows + 2 * IB, columns), jnp.bfloat16),
        name="join",
    )(*[pltpu.with_memory_space_constraint(piece, pltpu.VMEM) for piece in (first, second, third)])
    along_x = [[p * stride + g for p in range(KB)] for g in range(stride)]
    gathered = lax.all_to_all(
        message, "neu", 0, 0, axis_index_groups=along_x, tiled=True
    )
    share = columns // KB
    activations, sums = pl.pallas_call(
        layers_kernel,
        in_specs=[vmem],
        out_specs=[vmem, vmem],
        out_shape=[
            pltpu.VMEM((rows, columns), jnp.bfloat16),
            pltpu.VMEM((stride, 1, share), jnp.float32),
        ],
        scratch_shapes=[
            pltpu.VMEM((KB, rows, columns), jnp.bfloat16),
            pltpu.VMEM((KB, 1, share), jnp.float32),
        ],
        name="layers",
    )(pltpu.with_memory_space_constraint(gathered, pltpu.VMEM))
    across = [[p * stride + g for g in range(stride)] for p in range(KB)]
    parts = lax.all_to_all(sums, "neu", 0, 0, axis_index_groups=across, tiled=True)
    activations, totals = pl.pallas_call(
        finish_kernel,
        in_specs=[vmem, vmem],
        out_specs=[pl.BlockSpec(memory_space=pl.ANY)] * 2,
        out_shape=[
            jax.ShapeDtypeStruct((rows, columns), jnp.bfloat16),
            jax.ShapeDtypeStruct((1, columns // devices), jnp.float32),
        ],
        scratch_shapes=[
            pltpu.VMEM((1, columns // devices), jnp.float32),
            pltpu.SemaphoreType.DMA(()),
            pltpu.SemaphoreType.DMA(()),
        ],
        name="finish",
    )(
        pltpu.with_memory_space_constraint(parts, pltpu.VMEM),
        pltpu.with_memory_space_constraint(activations, pltpu.VMEM),
    )
    return activations, totals.reshape(-1)


def solution(mesh):
    in_specs = (P("neu", "img"), P("neu", "img"), P(None, "neu", None, None), P(None, "neu", None))
    out_specs = (P("neu", "img"), P(("img", "neu")))
    return jax.shard_map(
        on_device, mesh=mesh, in_specs=in_specs, out_specs=out_specs, check_vma=False
    )
```

```python
import jax
import jax.numpy as jnp
from jax import lax
from jax.experimental import pallas as pl
from jax.experimental.pallas import tpu as pltpu
from jax.sharding import PartitionSpec as P

KB = 4
IB = 8
OB = 32
LANES = 128
FIRST_X = 2

bias_value = 0.35
ceiling = 32.0


def from_group_ahead(block, axis, distance):
    devices = lax.axis_size(axis)
    groups = devices // KB
    route = [(i - i % groups + (i % groups + distance) % groups, i) for i in range(devices)]
    return lax.ppermute(block, axis, route)


def pack_kernel(values_ref, mask_ref, weights_ref, index_ref, first_ref, second_ref, third_ref):
    rows, columns = values_ref.shape
    outs = weights_ref.shape[-1]
    half = KB * outs
    run_blocks = rows // IB
    first_ref[0:rows, :] = values_ref[...] * mask_ref[...].astype(jnp.float32).astype(jnp.bfloat16)
    slot = lax.broadcasted_iota(jnp.int32, (IB, LANES), 0)
    out_block = lax.broadcasted_iota(jnp.int32, (IB, LANES), 1) // OB
    nothing = jnp.zeros((IB, LANES), jnp.float32)
    for layer in range(3):
        table = jnp.concatenate([weights_ref[layer, k].astype(jnp.float32) for k in range(KB)], axis=1)
        inner = jnp.zeros((IB, LANES), jnp.int32)
        for k in range(KB):
            for d in range(outs // OB):
                here = (slot == k + (KB if layer == 1 else 0)) & (out_block == d)
                inner = jnp.where(here, index_ref[layer, d, k] % run_blocks, inner)
        inner = inner.astype(jnp.float32)
        parts = [table, nothing, inner] if layer == 2 else [table, inner, nothing]
        packed = jnp.concatenate(parts, axis=1).astype(jnp.bfloat16)
        if layer == 0:
            first_ref[rows : rows + IB, :] = packed
        elif layer == 1:
            second_ref[...] = packed
        else:
            third_ref[...] = packed


def join_kernel(first_ref, second_ref, third_ref, message_ref):
    rows = first_ref.shape[0] - IB
    half = rows * KB
    for p in range(message_ref.shape[0]):
        message_ref[p, 0:rows, :] = first_ref[0:rows, :]
        message_ref[p, rows : rows + IB, 0:half] = first_ref[rows : rows + IB, 0:half]
        message_ref[p, rows : rows + IB, half:] = second_ref[:, 0:half]
        message_ref[p, rows + IB :, 0:half] = third_ref[:, 0:half]
        message_ref[p, rows + IB :, half : half + LANES] = (
            first_ref[rows : rows + IB, half : half + LANES] + second_ref[:, half : half + LANES]
        )
        message_ref[p, rows + IB :, half + LANES :] = third_ref[:, half + LANES :]


def dense_transposed(gathered_ref, layer, outs, positions, run_blocks):
    half = KB * outs
    table_row, table_lane, index_lane, index_row = (
        (outs, 0, half, 0),
        (outs, half, half, KB),
        (outs + IB, 0, half + LANES, 0),
    )[layer]
    tables = [
        gathered_ref[p, table_row : table_row + IB, table_lane : table_lane + half].astype(jnp.float32)
        for p in range(positions)
    ]
    inner = [
        gathered_ref[p, outs + IB : outs + 2 * IB, index_lane : index_lane + LANES].astype(jnp.float32)
        for p in range(positions)
    ]
    rows = []
    for source in range(positions):
        w_parts, i_parts = [], []
        for target in range(positions):
            k = (source - target) % positions
            w_parts.append(tables[target][:, k * outs : (k + 1) * outs])
            i_parts.append(inner[target][index_row + k : index_row + k + 1, 0:outs])
        w_row = jnp.concatenate(w_parts, axis=1)
        i_row = jnp.broadcast_to(jnp.concatenate(i_parts, axis=1), w_row.shape)
        for b in range(run_blocks):
            rows.append(jnp.where(i_row == float(b), w_row, 0.0))
    return jnp.concatenate(rows, axis=0).astype(jnp.bfloat16)


def advance(dense_t, activity):
    summed = lax.dot_general(
        dense_t, activity, (((0,), (0,)), ((), ())), preferred_element_type=jnp.float32
    )
    return jnp.minimum(jnp.maximum(summed - bias_value, 0.0), ceiling).astype(jnp.bfloat16)


def layers_kernel(gathered_ref, activations_ref, sums_ref, last_ref, totals_ref):
    positions, _, columns = gathered_ref.shape
    rows = activations_ref.shape[0]
    run_blocks = rows // IB
    groups = lax.axis_size("neu") // KB
    place = lax.axis_index("neu") // groups
    group = lax.axis_index("neu") % groups
    wraps = (None, group == groups - 3, group >= groups - 2)
    activity = jnp.concatenate([gathered_ref[p, 0:rows, :] for p in range(positions)], axis=0)
    for layer in range(3):
        dense_t = dense_transposed(gathered_ref, layer, rows, positions, run_blocks)
        if layer > 0:
            further = jnp.concatenate([activity[rows:], activity[:rows]], axis=0)
            activity = jnp.where(wraps[layer], further, activity)
        activity = advance(dense_t, activity)
    last_ref[...] = activity.reshape(positions, rows, columns)
    activations_ref[...] = last_ref[(place + KB - FIRST_X) % KB]
    totals = jnp.sum(activity.astype(jnp.float32), axis=0, keepdims=True)
    share = columns // positions
    for p in range(positions):
        totals_ref[p] = totals[:, p * share : (p + 1) * share]
    sums_ref[...] = jnp.broadcast_to(totals_ref[place][None], sums_ref.shape)


def finish_kernel(parts_ref, run_ref, activations_ref, totals_ref, own_ref, copied, summed):
    out = pltpu.make_async_copy(run_ref, activations_ref, copied)
    out.start()
    share = parts_ref.shape[-1]
    own = totals_ref.shape[-1]
    begin = (lax.axis_index("neu") % parts_ref.shape[0]) * own
    totals = jnp.broadcast_to(jnp.sum(parts_ref[...], axis=0), (8, share))
    own_ref[...] = pltpu.roll(totals, (share - begin) % share, 1)[0:1, 0:own]
    own_out = pltpu.make_async_copy(own_ref, totals_ref, summed)
    own_out.start()
    out.wait()
    own_out.wait()


def on_device(image_values, image_mask, weights, block_index):
    rows, columns = image_values.shape
    devices = lax.axis_size("neu")
    stride = devices // KB
    layer_count = weights.shape[0]
    vmem = pl.BlockSpec(memory_space=pltpu.VMEM)
    smem = pl.BlockSpec(memory_space=pltpu.SMEM)
    first, second, third = pl.pallas_call(
        pack_kernel,
        in_specs=[vmem, vmem, vmem, smem],
        out_specs=[vmem, vmem, vmem],
        out_shape=[
            pltpu.VMEM((rows + IB, columns), jnp.bfloat16),
            pltpu.VMEM((IB, columns), jnp.bfloat16),
            pltpu.VMEM((IB, columns), jnp.bfloat16),
        ],
        name="pack",
    )(image_values, image_mask, weights.transpose(0, 2, 3, 1), block_index)
    first = from_group_ahead(first, "neu", 3)
    second = from_group_ahead(second, "neu", 2)
    message = pl.pallas_call(
        join_kernel,
        in_specs=[vmem] * 3,
        out_specs=vmem,
        out_shape=pltpu.VMEM((KB, rows + 2 * IB, columns), jnp.bfloat16),
        name="join",
    )(*[pltpu.with_memory_space_constraint(piece, pltpu.VMEM) for piece in (first, second, third)])
    along_x = [[(p + FIRST_X) % KB * stride + g for p in range(KB)] for g in range(stride)]
    gathered = lax.all_to_all(
        message, "neu", 0, 0, axis_index_groups=along_x, tiled=True
    )
    share = columns // KB
    activations, sums = pl.pallas_call(
        layers_kernel,
        in_specs=[vmem],
        out_specs=[vmem, vmem],
        out_shape=[
            pltpu.VMEM((rows, columns), jnp.bfloat16),
            pltpu.VMEM((stride, 1, share), jnp.float32),
        ],
        scratch_shapes=[
            pltpu.VMEM((KB, rows, columns), jnp.bfloat16),
            pltpu.VMEM((KB, 1, share), jnp.float32),
        ],
        name="layers",
    )(pltpu.with_memory_space_constraint(gathered, pltpu.VMEM))
    farthest = stride // 2 + 1
    across = [[p * stride + (g + farthest) % stride for g in range(stride)] for p in range(KB)]
    parts = lax.all_to_all(sums, "neu", 0, 0, axis_index_groups=across, tiled=True)
    activations, totals = pl.pallas_call(
        finish_kernel,
        in_specs=[vmem, vmem],
        out_specs=[pl.BlockSpec(memory_space=pl.ANY)] * 2,
        out_shape=[
            jax.ShapeDtypeStruct((rows, columns), jnp.bfloat16),
            jax.ShapeDtypeStruct((1, columns // devices), jnp.float32),
        ],
        scratch_shapes=[
            pltpu.VMEM((1, columns // devices), jnp.float32),
            pltpu.SemaphoreType.DMA(()),
            pltpu.SemaphoreType.DMA(()),
        ],
        name="finish",
    )(
        pltpu.with_memory_space_constraint(parts, pltpu.VMEM),
        pltpu.with_memory_space_constraint(activations, pltpu.VMEM),
    )
    return activations, totals.reshape(-1)


def solution(mesh):
    in_specs = (P("neu", "img"), P("neu", "img"), P(None, "neu", None, None), P(None, "neu", None))
    out_specs = (P("neu", "img"), P(("img", "neu")))
    return jax.shard_map(
        on_device, mesh=mesh, in_specs=in_specs, out_specs=out_specs, check_vma=False
    )
```

```python
import jax
import jax.numpy as jnp
from jax import lax
from jax.experimental import pallas as pl
from jax.experimental.pallas import tpu as pltpu
from jax.sharding import PartitionSpec as P

KB = 4
IB = 8
OB = 32
LANES = 128
ALONG_X = (2, 1, 3, 0)

bias_value = 0.35
ceiling = 32.0


def from_group_ahead(block, axis, distance):
    devices = lax.axis_size(axis)
    groups = devices // KB
    route = [(i - i % groups + (i % groups + distance) % groups, i) for i in range(devices)]
    return lax.ppermute(block, axis, route)


def pack_kernel(values_ref, mask_ref, weights_ref, index_ref, first_ref, second_ref, third_ref):
    rows, columns = values_ref.shape
    outs = weights_ref.shape[-1]
    half = KB * outs
    run_blocks = rows // IB
    first_ref[0:rows, :] = values_ref[...] * mask_ref[...].astype(jnp.float32).astype(jnp.bfloat16)
    slot = lax.broadcasted_iota(jnp.int32, (IB, LANES), 0)
    out_block = lax.broadcasted_iota(jnp.int32, (IB, LANES), 1) // OB
    nothing = jnp.zeros((IB, LANES), jnp.float32)
    for layer in range(3):
        table = jnp.concatenate([weights_ref[layer, k].astype(jnp.float32) for k in range(KB)], axis=1)
        inner = jnp.zeros((IB, LANES), jnp.int32)
        for k in range(KB):
            for d in range(outs // OB):
                here = (slot == k + (KB if layer == 1 else 0)) & (out_block == d)
                inner = jnp.where(here, index_ref[layer, d, k] % run_blocks, inner)
        inner = inner.astype(jnp.float32)
        parts = [table, nothing, inner] if layer == 2 else [table, inner, nothing]
        packed = jnp.concatenate(parts, axis=1).astype(jnp.bfloat16)
        if layer == 0:
            first_ref[rows : rows + IB, :] = packed
        elif layer == 1:
            second_ref[...] = packed
        else:
            third_ref[...] = packed


def join_kernel(first_ref, second_ref, third_ref, message_ref):
    rows = first_ref.shape[0] - IB
    half = rows * KB
    for p in range(message_ref.shape[0]):
        message_ref[p, 0:rows, :] = first_ref[0:rows, :]
        message_ref[p, rows : rows + IB, 0:half] = first_ref[rows : rows + IB, 0:half]
        message_ref[p, rows : rows + IB, half:] = second_ref[:, 0:half]
        message_ref[p, rows + IB :, 0:half] = third_ref[:, 0:half]
        message_ref[p, rows + IB :, half : half + LANES] = (
            first_ref[rows : rows + IB, half : half + LANES] + second_ref[:, half : half + LANES]
        )
        message_ref[p, rows + IB :, half + LANES :] = third_ref[:, half + LANES :]


def dense_transposed(gathered_ref, layer, outs, positions, run_blocks):
    half = KB * outs
    table_row, table_lane, index_lane, index_row = (
        (outs, 0, half, 0),
        (outs, half, half, KB),
        (outs + IB, 0, half + LANES, 0),
    )[layer]
    tables = [
        gathered_ref[p, table_row : table_row + IB, table_lane : table_lane + half].astype(jnp.float32)
        for p in range(positions)
    ]
    inner = [
        gathered_ref[p, outs + IB : outs + 2 * IB, index_lane : index_lane + LANES].astype(jnp.float32)
        for p in range(positions)
    ]
    rows = []
    for source in range(positions):
        w_parts, i_parts = [], []
        for target in range(positions):
            k = (ALONG_X[source] - ALONG_X[target]) % positions
            w_parts.append(tables[target][:, k * outs : (k + 1) * outs])
            i_parts.append(inner[target][index_row + k : index_row + k + 1, 0:outs])
        w_row = jnp.concatenate(w_parts, axis=1)
        i_row = jnp.broadcast_to(jnp.concatenate(i_parts, axis=1), w_row.shape)
        for b in range(run_blocks):
            rows.append(jnp.where(i_row == float(b), w_row, 0.0))
    return jnp.concatenate(rows, axis=0).astype(jnp.bfloat16)


def advance(dense_t, activity):
    summed = lax.dot_general(
        dense_t, activity, (((0,), (0,)), ((), ())), preferred_element_type=jnp.float32
    )
    return jnp.minimum(jnp.maximum(summed - bias_value, 0.0), ceiling).astype(jnp.bfloat16)


def layers_kernel(gathered_ref, activations_ref, sums_ref, last_ref, totals_ref):
    positions, _, columns = gathered_ref.shape
    rows = activations_ref.shape[0]
    run_blocks = rows // IB
    groups = lax.axis_size("neu") // KB
    place = lax.axis_index("neu") // groups
    group = lax.axis_index("neu") % groups
    wraps = (None, group == groups - 3, group >= groups - 2)
    activity = jnp.concatenate([gathered_ref[p, 0:rows, :] for p in range(positions)], axis=0)
    for layer in range(3):
        dense_t = dense_transposed(gathered_ref, layer, rows, positions, run_blocks)
        if layer > 0:
            nexts = [ALONG_X.index((x + 1) % positions) for x in ALONG_X]
            further = jnp.concatenate([activity[p * rows : (p + 1) * rows] for p in nexts], axis=0)
            activity = jnp.where(wraps[layer], further, activity)
        activity = advance(dense_t, activity)
    last_ref[...] = activity.reshape(positions, rows, columns)
    position = 0
    for p in range(1, positions):
        position = jnp.where(place == ALONG_X[p], p, position)
    activations_ref[...] = last_ref[position]
    totals = jnp.sum(activity.astype(jnp.float32), axis=0, keepdims=True)
    share = columns // positions
    for p in range(positions):
        totals_ref[p] = totals[:, p * share : (p + 1) * share]
    sums_ref[...] = jnp.broadcast_to(totals_ref[place][None], sums_ref.shape)


def finish_kernel(parts_ref, run_ref, activations_ref, totals_ref, own_ref, copied, summed):
    out = pltpu.make_async_copy(run_ref, activations_ref, copied)
    out.start()
    share = parts_ref.shape[-1]
    own = totals_ref.shape[-1]
    begin = (lax.axis_index("neu") % parts_ref.shape[0]) * own
    totals = jnp.broadcast_to(jnp.sum(parts_ref[...], axis=0), (8, share))
    own_ref[...] = pltpu.roll(totals, (share - begin) % share, 1)[0:1, 0:own]
    own_out = pltpu.make_async_copy(own_ref, totals_ref, summed)
    own_out.start()
    out.wait()
    own_out.wait()


def on_device(image_values, image_mask, weights, block_index):
    rows, columns = image_values.shape
    devices = lax.axis_size("neu")
    stride = devices // KB
    layer_count = weights.shape[0]
    vmem = pl.BlockSpec(memory_space=pltpu.VMEM)
    smem = pl.BlockSpec(memory_space=pltpu.SMEM)
    first, second, third = pl.pallas_call(
        pack_kernel,
        in_specs=[vmem, vmem, vmem, smem],
        out_specs=[vmem, vmem, vmem],
        out_shape=[
            pltpu.VMEM((rows + IB, columns), jnp.bfloat16),
            pltpu.VMEM((IB, columns), jnp.bfloat16),
            pltpu.VMEM((IB, columns), jnp.bfloat16),
        ],
        name="pack",
    )(image_values, image_mask, weights.transpose(0, 2, 3, 1), block_index)
    first = from_group_ahead(first, "neu", 3)
    second = from_group_ahead(second, "neu", 2)
    message = pl.pallas_call(
        join_kernel,
        in_specs=[vmem] * 3,
        out_specs=vmem,
        out_shape=pltpu.VMEM((KB, rows + 2 * IB, columns), jnp.bfloat16),
        name="join",
    )(*[pltpu.with_memory_space_constraint(piece, pltpu.VMEM) for piece in (first, second, third)])
    along_x = [[x * stride + g for x in ALONG_X] for g in range(stride)]
    gathered = lax.all_to_all(
        message, "neu", 0, 0, axis_index_groups=along_x, tiled=True
    )
    share = columns // KB
    activations, sums = pl.pallas_call(
        layers_kernel,
        in_specs=[vmem],
        out_specs=[vmem, vmem],
        out_shape=[
            pltpu.VMEM((rows, columns), jnp.bfloat16),
            pltpu.VMEM((stride, 1, share), jnp.float32),
        ],
        scratch_shapes=[
            pltpu.VMEM((KB, rows, columns), jnp.bfloat16),
            pltpu.VMEM((KB, 1, share), jnp.float32),
        ],
        name="layers",
    )(pltpu.with_memory_space_constraint(gathered, pltpu.VMEM))
    farthest = stride // 2 + 1
    across = [[p * stride + (g + farthest) % stride for g in range(stride)] for p in range(KB)]
    parts = lax.all_to_all(sums, "neu", 0, 0, axis_index_groups=across, tiled=True)
    activations, totals = pl.pallas_call(
        finish_kernel,
        in_specs=[vmem, vmem],
        out_specs=[pl.BlockSpec(memory_space=pl.ANY)] * 2,
        out_shape=[
            jax.ShapeDtypeStruct((rows, columns), jnp.bfloat16),
            jax.ShapeDtypeStruct((1, columns // devices), jnp.float32),
        ],
        scratch_shapes=[
            pltpu.VMEM((1, columns // devices), jnp.float32),
            pltpu.SemaphoreType.DMA(()),
            pltpu.SemaphoreType.DMA(()),
        ],
        name="finish",
    )(
        pltpu.with_memory_space_constraint(parts, pltpu.VMEM),
        pltpu.with_memory_space_constraint(activations, pltpu.VMEM),
    )
    return activations, totals.reshape(-1)


def solution(mesh):
    in_specs = (P("neu", "img"), P("neu", "img"), P(None, "neu", None, None), P(None, "neu", None))
    out_specs = (P("neu", "img"), P(("img", "neu")))
    return jax.shard_map(
        on_device, mesh=mesh, in_specs=in_specs, out_specs=out_specs, check_vma=False
    )
```
